32 devices in a mesh: wave: 16 (over z, y, x), field: 2 (over core).
Axes of the slice: x: 2, y: 2, z: 4, core: 2. Of those that a mesh axis runs over, the one named last changes fastest.
Arguments:
- right_vector: float32 [4, 3, 512, 2, 512], P('field', None, 'wave'), may hold values from -8 to 8
- left_prev: float32 [4, 3, 512, 2, 512], P('field', None, 'wave'), may hold values from -6 to 6
- beta_prev: float32 [1], replicated, may hold values from 0.5 to 2
- kept_vectors: bfloat16 [20, 4, 3, 512, 2, 512], P(None, 'field', None, 'wave'), may hold values from -8 to 8
- kept_count: int32 [1], replicated, may hold values from 1 to 20
- wave_table: int32 [512], replicated, may hold values from 0 to 511, each once
- legendre: float32 [512, 512, 512], P('wave'), may hold values from -0.25 to 0.25
- quad_weights: float32 [512], replicated, may hold values from 0.2 to 1
- coef_value: bfloat16 [3, 3, 512, 1024], P(None, None, 'wave'), may hold values from -2.390625 to 2.390625
- coef_zonal: bfloat16 [3, 3, 512, 1024], P(None, None, 'wave'), may hold values from -2.390625 to 2.390625
Outputs:
- left_vector: float32 [4, 3, 512, 2, 512], P('field', None, 'wave')
- right_next: float32 [4, 3, 512, 2, 512], P('field', None, 'wave')
- correlations: float32 [20], replicated
- norms: float32 [2], replicated
The draws below stay inside these ranges and needn't reach their ends.
Inputs may be any that keep to these rules, and one draw needn't show every extreme that they name: The stored vectors numbered below kept_count take part. A permutation: spectral slot s holds zonal wavenumber wave_table[s].
All inputs are finite; a program needn't handle non-finite values.
Results may differ from the reference program's by a relative error of at most 0.0003.
Values sent between devices are 32-bit elements; how exact they have to be, the bound alone decides.
A program may use at most 192 MiB of HBM per device.

```python
import math
import jax
import jax.numpy as jnp
from jax import lax

M = 512
NLAT = 512
NLON = 1024
FIELDS = 3
KEEP = 20
LEVELS = 4


def shared_base(key):
    values = jax.random.normal(jax.random.fold_in(key, 101), (LEVELS, FIELDS, M, 2, M), jnp.float32)
    return values


def draw_right_vector(key, part):
    shared = shared_base(key)
    noise_part = jax.random.normal(jax.random.fold_in(key, 211), shared.shape, jnp.float32)
    return jnp.clip(shared + 0.3 * noise_part, -8.0, 8.0)


def draw_kept_vectors(key, part):
    shared = shared_base(key)
    mix_weights = jax.random.uniform(jax.random.fold_in(key, 307), (KEEP, 1, 1, 1, 1, 1), jnp.float32, 0.1, 0.4)
    noise_part = jax.random.normal(jax.random.fold_in(key, 401), (KEEP,) + shared.shape, jnp.float32)
    mixed = mix_weights * shared[None] + jnp.sqrt(1.0 - mix_weights * mix_weights) * noise_part
    return jnp.clip(mixed, -8.0, 8.0).astype(jnp.bfloat16)


def block_scale(own_key, shape, shards, smallest, top_value):
    gain, own = 1.0, jax.random.fold_in(own_key, 6)
    for axis_at, shards_of in shards:
        steps = jnp.exp(jax.random.uniform(jax.random.fold_in(own, axis_at), (shards_of,), jnp.float32, smallest / len(shards), top_value / len(shards)))
        gain = gain * jnp.repeat(steps, shape[axis_at] // shards_of).reshape([-1 if axis == axis_at else 1 for axis in range(len(shape))])
    return gain


def gaussian(stream_key, dims, scale, limit, pieces=(), kind=jnp.bfloat16):
    factor_of = block_scale(stream_key, dims, pieces, -0.22, 0.18) if pieces else 1.0
    drawn = jax.random.normal(stream_key, dims, jnp.float32) * scale * factor_of
    return jnp.minimum(jnp.maximum(drawn, -limit), limit).astype(kind)


def setup_inputs(seed: int = 0) -> dict:
    key_list = jax.random.split(jax.random.key(seed), 11)
    right_vector = draw_right_vector(jax.random.fold_in(key_list[10], 71), 0)
    left_prev = gaussian(key_list[1], (LEVELS, FIELDS, M, 2, M), 1.0, 6.0, ((0, 2), (2, 16)), jnp.float32)
    beta_prev = jnp.clip(jax.random.uniform(key_list[2], (1,), jnp.float32, 0.5, 2.0), 0.5, 2.0)
    kept_vectors = draw_kept_vectors(jax.random.fold_in(key_list[10], 71), 0)
    kept_count = jax.random.randint(key_list[4], (1,), 1, KEEP + 1).astype(jnp.int32)
    wave_table = jax.random.permutation(key_list[5], M).astype(jnp.int32)
    legendre = gaussian(key_list[6], (M, M, NLAT), M ** -0.5, 0.25, ((0, 16),), jnp.float32)
    quad_weights = jnp.clip(jnp.exp(jax.random.uniform(key_list[7], (NLAT,), jnp.float32, math.log(0.2), math.log(1.0))), 0.2, 1.0)
    coef_value = gaussian(key_list[8], (FIELDS, FIELDS, NLAT, NLON), 0.4, 2.390625, ((2, 16),))
    coef_zonal = gaussian(key_list[9], (FIELDS, FIELDS, NLAT, NLON), 0.4, 2.390625, ((2, 16),))
    return {"right_vector": right_vector, "left_prev": left_prev, "beta_prev": beta_prev, "kept_vectors": kept_vectors, "kept_count": kept_count, "wave_table": wave_table, "legendre": legendre, "quad_weights": quad_weights, "coef_value": coef_value, "coef_zonal": coef_zonal}


time_step = 0.5
epsilon = 1e-06
highest = lax.Precision.HIGHEST

def to_latitudes(spectral, legendre):
    return jnp.einsum('lfsrn,snt->lfsrt', spectral, legendre, precision=highest)

def to_degrees(latitude_part, legendre):
    return jnp.einsum('lfsrt,snt->lfsrn', latitude_part, legendre, precision=highest)

def wave_sum(real_part, imag_part, wave_table):
    combined = lax.complex(real_part, imag_part)
    spectrum = jnp.zeros(combined.shape[:-1] + (NLON,), combined.dtype).at[..., wave_table].set(combined)
    return jnp.real(jnp.fft.ifft(spectrum, axis=-1)) * NLON

def wave_parts(grid_field, wave_table):
    spectrum = jnp.fft.fft(grid_field, axis=-1)[..., wave_table]
    return (jnp.real(spectrum), jnp.imag(spectrum))

def to_slots(real_part, imag_part):
    return jnp.stack([real_part, imag_part], axis=-1).transpose(0, 1, 3, 4, 2)

def reference(right_vector, left_prev, beta_prev, kept_vectors, kept_count, wave_table, legendre, quad_weights, coef_value, coef_zonal):
    degree_ids = jnp.arange(M, dtype=jnp.int32)
    live_mask = (degree_ids[None, :] >= wave_table[:, None]).astype(jnp.float32)[None, None, :, None, :]
    waves_float = wave_table.astype(jnp.float32)
    value_coef = coef_value.astype(jnp.float32)
    zonal_coef = coef_zonal.astype(jnp.float32)
    weights = quad_weights[None, None, :, None]
    right_live = right_vector * live_mask
    prev_live = left_prev * live_mask
    latitude_part = to_latitudes(right_live, legendre)
    real_part = jnp.swapaxes(latitude_part[:, :, :, 0, :], 2, 3)
    imag_part = jnp.swapaxes(latitude_part[:, :, :, 1, :], 2, 3)
    values = wave_sum(real_part, imag_part, wave_table) * M ** (-0.5)
    slopes = wave_sum(-waves_float * imag_part, waves_float * real_part, wave_table) * M ** (-1.5)
    tendency = jnp.einsum('fgtx,lgtx->lftx', value_coef, values, precision=highest)
    tendency = tendency + jnp.einsum('fgtx,lgtx->lftx', zonal_coef, slopes, precision=highest)
    real_out, imag_out = wave_parts(tendency * weights, wave_table)
    grid_scale = NLON ** (-0.5)
    forward_image = to_degrees(to_slots(real_out * grid_scale, imag_out * grid_scale), legendre) * live_mask
    residual_left = right_live + time_step * forward_image - beta_prev[0] * prev_live
    alpha_norm = jnp.sqrt(jnp.mean(residual_left * residual_left) + epsilon)
    left_vector = residual_left / alpha_norm
    latitude_back = to_latitudes(left_vector, legendre)
    real_part = jnp.swapaxes(latitude_back[:, :, :, 0, :], 2, 3)
    imag_part = jnp.swapaxes(latitude_back[:, :, :, 1, :], 2, 3)
    spread = wave_sum(real_part, imag_part, wave_table) * grid_scale * weights
    value_part = jnp.einsum('fgtx,lftx->lgtx', value_coef, spread, precision=highest)
    zonal_part = jnp.einsum('fgtx,lftx->lgtx', zonal_coef, spread, precision=highest)
    value_real, value_imag = wave_parts(value_part, wave_table)
    zonal_real, zonal_imag = wave_parts(zonal_part, wave_table)
    root_scale = M ** (-0.5)
    slope_scale = waves_float / M
    back_real = root_scale * (value_real + slope_scale * zonal_imag)
    back_imag = root_scale * (value_imag - slope_scale * zonal_real)
    returned = to_degrees(to_slots(back_real, back_imag), legendre) * live_mask
    candidate = left_vector + time_step * returned - alpha_norm * right_live
    live_flags = (jnp.arange(KEEP, dtype=jnp.int32) < kept_count[0]).astype(jnp.float32)

    def correlation_one(kept_one):
        return jnp.mean(kept_one.astype(jnp.float32) * live_mask * candidate)
    raw_correlation = lax.map(correlation_one, kept_vectors)
    correlations = raw_correlation * live_flags

    def add_one(running, members):
        kept_one, weight_one = members
        return (running + weight_one * (kept_one.astype(jnp.float32) * live_mask), None)
    correction, unused = lax.scan(add_one, jnp.zeros_like(candidate), (kept_vectors, correlations))
    orthogonal = candidate - correction
    beta_norm = jnp.sqrt(jnp.mean(orthogonal * orthogonal) + epsilon)
    return (left_vector, orthogonal / beta_norm, correlations, jnp.stack([alpha_norm, beta_norm]))
```

```python
import functools
import math

import jax
import jax.numpy as jnp
from jax import lax
from jax.experimental import pallas as pl
from jax.experimental.pallas import tpu as pltpu
from jax.sharding import PartitionSpec as P

time_step = 0.5
epsilon = 1e-06
f32 = jnp.float32
bf16 = jnp.bfloat16


def split(x):
    high = x.astype(bf16)
    return high, (x - high.astype(f32)).astype(bf16)


def dot(a, b, contract):
    return lax.dot_general(a, b, (((1,), (contract,)), ((), ())), preferred_element_type=f32)


def split_dot(rows, b_high, b_low, contract):
    count = rows.shape[0]
    high = rows.astype(bf16).astype(f32)
    both = jnp.concatenate([high, rows - high], axis=0).astype(bf16)
    upper = dot(both, b_high, contract)
    lower = dot(both[:count], b_low, contract)
    return upper[:count] + (upper[count:] + lower)


def table_kernel(longitudes, waves_ref, high_ref, low_ref):
    rows, width = high_ref.shape
    column = lax.broadcasted_iota(jnp.int32, (rows, width), 1)
    shift = jnp.where(pl.program_id(0) < pl.num_programs(0) // 2, 0, longitudes // 4)
    phase = lax.rem(waves_ref[...] * column + shift, longitudes)
    turn = phase.astype(f32) * (4.0 / longitudes)
    quadrant = jnp.floor(turn + 0.5)
    angle = (turn - quadrant) * (0.5 * math.pi)
    quadrant = quadrant.astype(jnp.int32) & 3
    square = angle * angle
    sine = angle * (
        1.0 + square * (-1 / 6 + square * (1 / 120 + square * (-1 / 5040 + square / 362880)))
    )
    cosine = 1.0 + square * (
        -0.5 + square * (1 / 24 + square * (-1 / 720 + square * (1 / 40320 - square / 3628800)))
    )
    value = jnp.where((quadrant & 1) == 1, sine, cosine)
    value = jnp.where((quadrant == 1) | (quadrant == 2), -value, value)
    high, low = split(value)
    high_ref[...] = high
    low_ref[...] = low


def fourier_table(wave_table, longitudes):
    slots = wave_table.shape[0]
    waves = jnp.concatenate([wave_table, wave_table])[:, None]
    block = slots // 4
    out = jax.ShapeDtypeStruct((2 * slots, longitudes), bf16)
    return pl.pallas_call(
        functools.partial(table_kernel, longitudes),
        grid=(8,),
        in_specs=[pl.BlockSpec((block, 1), lambda i: (i, 0))],
        out_specs=[pl.BlockSpec((block, longitudes), lambda i: (i, 0))] * 2,
        out_shape=[out, out],
        name="table",
    )(waves)


def legendre_kernel(mode, block, waves_ref, beta_ref, *refs):
    refs = list(refs)
    basis_ref = refs.pop(0)
    spectral_ref = refs.pop(0)
    prev_ref = refs.pop(0) if mode == "both" else None
    image_ref = refs.pop(0) if mode != "synthesis" else None
    new_ref = refs.pop(0) if mode != "synthesis" else None
    out_ref = refs.pop(0) if mode != "analysis" else None
    rows_ref = refs.pop(0)
    gather_ref = refs.pop(0) if mode != "synthesis" else None
    acc_ref = refs.pop(0) if mode != "analysis" else None
    levels, fields = spectral_ref.shape[:2]
    parts = spectral_ref.shape[3]
    degrees = basis_ref.shape[1]
    used = levels * fields * parts
    step = pl.program_id(0)
    waves_dev = pl.num_programs(0) * block

    @pl.when(step == 0)
    def _():
        rows_ref[...] = jnp.zeros_like(rows_ref)
        if gather_ref is not None:
            gather_ref[...] = image_ref[...].T

    for j in range(block):
        slot = step * block + j
        degree = lax.broadcasted_iota(jnp.int32, (rows_ref.shape[1], degrees), 1)
        mask = (degree >= waves_ref[slot]).astype(f32)

        def pack(which, ref):
            for l in range(levels):
                for f in range(fields):
                    at = (l * fields + f) * parts
                    rows_ref[which, pl.ds(at, parts), :] = ref[l, f, j]

        pack(0, spectral_ref)
        current = rows_ref[0] * mask
        high, low = split(basis_ref[j])
        if mode != "synthesis":
            for i in range(used):
                rows_ref[1, pl.ds(i, 1), :] = gather_ref[pl.ds(i * waves_dev + slot, 1), :]
            image = split_dot(rows_ref[1], high, low, 1) * mask
            current = current + time_step * image
            if mode == "both":
                pack(2, prev_ref)
                current = current - beta_ref[0] * (rows_ref[2] * mask)
            for l in range(levels):
                for f in range(fields):
                    at = (l * fields + f) * parts
                    new_ref[l, f, j] = current[at : at + parts]
        if mode != "analysis":
            result = split_dot(current, high, low, 0)
            for i in range(used):
                acc_ref[pl.ds(i * waves_dev + slot, 1), :] = result[i : i + 1]

    if mode != "analysis":

        @pl.when(step == pl.num_programs(0) - 1)
        def _():
            out_ref[...] = acc_ref[...].T


def legendre_call(mode, waves, beta, basis, spectral, prev=None, image=None):
    levels, fields, waves_dev, parts, degrees = spectral.shape
    latitudes = basis.shape[2]
    used = levels * fields * parts
    padded = -(-used // 16) * 16
    block = 2 if waves_dev % 2 == 0 else 1
    spec = pl.BlockSpec((levels, fields, block, parts, degrees), lambda s, *_: (0, 0, s, 0, 0))
    whole = pl.BlockSpec((latitudes, used * waves_dev), lambda s, *_: (0, 0))
    operands = [basis, spectral]
    in_specs = [pl.BlockSpec((block, degrees, latitudes), lambda s, *_: (s, 0, 0)), spec]
    out_specs, out_shape = [], []
    scratch = [pltpu.VMEM((3, padded, degrees), f32)]
    lanes = pltpu.VMEM((used * waves_dev, latitudes), f32)
    if mode == "both":
        operands.append(prev)
        in_specs.append(spec)
    if mode != "synthesis":
        operands.append(image)
        in_specs.append(whole)
        out_specs.append(spec)
        out_shape.append(jax.ShapeDtypeStruct(spectral.shape, f32))
        scratch.append(lanes)
    if mode != "analysis":
        out_specs.append(whole)
        out_shape.append(jax.ShapeDtypeStruct((latitudes, used * waves_dev), f32))
        scratch.append(lanes)
    return pl.pallas_call(
        functools.partial(legendre_kernel, mode, block),
        grid_spec=pltpu.PrefetchScalarGridSpec(
            num_scalar_prefetch=2,
            grid=(waves_dev // block,),
            in_specs=in_specs,
            out_specs=out_specs,
            scratch_shapes=scratch,
        ),
        out_shape=out_shape,
        compiler_params=pltpu.CompilerParams(vmem_limit_bytes=40 * 1024 * 1024),
        name=mode,
    )(waves, beta, *operands)


def fourier_kernel(
    adjoint, levels, fields, block_ref, scale_ref, weight_ref, high_ref, low_ref, value_ref,
    zonal_ref, out_ref, coef_ref, left_ref, right_ref, acc_ref,
):
    groups, lat_dev, columns = block_ref.shape
    items = levels * fields
    waves_dev = columns // (2 * items)
    slots = groups * waves_dev
    rows = items * lat_dev
    step = pl.program_id(0)

    @pl.when(step == 0)
    def _():
        for w in range(groups):
            for i in range(items):
                for r in range(2):
                    coef_ref[
                        pl.ds(i * lat_dev, lat_dev), pl.ds(r * slots + w * waves_dev, waves_dev)
                    ] = block_ref[w, :, pl.ds((2 * i + r) * waves_dev, waves_dev)]
        if not adjoint:
            scale = scale_ref[...]
            coef_ref[pl.ds(rows, rows), pl.ds(0, slots)] = (
                -scale * coef_ref[pl.ds(0, rows), pl.ds(slots, slots)]
            )
            coef_ref[pl.ds(rows, rows), pl.ds(slots, slots)] = (
                scale * coef_ref[pl.ds(0, rows), pl.ds(0, slots)]
            )
        acc_ref[...] = jnp.zeros_like(acc_ref)

    high, low = high_ref[...], low_ref[...]
    left_ref[...] = split_dot(coef_ref[...], high, low, 0)
    weight = weight_ref[...]
    for l in range(levels):
        base = l * fields
        if adjoint:
            grid = [left_ref[pl.ds((base + f) * lat_dev, lat_dev), :] * weight for f in range(fields)]
            for g in range(fields):
                for k, ref in enumerate((value_ref, zonal_ref)):
                    total = sum(ref[f, g].astype(f32) * grid[f] for f in range(fields))
                    right_ref[pl.ds(k * rows + (base + g) * lat_dev, lat_dev), :] = total
        else:
            value = [left_ref[pl.ds((base + g) * lat_dev, lat_dev), :] for g in range(fields)]
            slope = [left_ref[pl.ds(rows + (base + g) * lat_dev, lat_dev), :] for g in range(fields)]
            for f in range(fields):
                total = sum(
                    value_ref[f, g].astype(f32) * value[g] + zonal_ref[f, g].astype(f32) * slope[g]
                    for g in range(fields)
                )
                right_ref[pl.ds((base + f) * lat_dev, lat_dev), :] = total * weight
    acc_ref[...] += split_dot(right_ref[...], high, low, 1)

    @pl.when(step == pl.num_programs(0) - 1)
    def _():
        if adjoint:
            scale = scale_ref[...]
            first = pl.ds(0, rows)
            second = pl.ds(rows, rows)
            acc_ref[first, pl.ds(0, slots)] += scale * acc_ref[second, pl.ds(slots, slots)]
            acc_ref[first, pl.ds(slots, slots)] -= scale * acc_ref[second, pl.ds(0, slots)]
        for w in range(groups):
            for i in range(items):
                for r in range(2):
                    out_ref[w, :, pl.ds((2 * i + r) * waves_dev, waves_dev)] = acc_ref[
                        pl.ds(i * lat_dev, lat_dev), pl.ds(r * slots + w * waves_dev, waves_dev)
                    ]


def fourier_call(adjoint, levels, fields, block, scale, weight, table, value, zonal):
    groups, lat_dev, columns = block.shape
    high, low = table
    slots2, longitudes = high.shape
    chunk = 256
    rows = levels * fields * lat_dev
    before, after = (rows, 2 * rows) if adjoint else (2 * rows, rows)
    coef_spec = pl.BlockSpec((fields, fields, lat_dev, chunk), lambda c: (0, 0, 0, c))
    table_spec = pl.BlockSpec((slots2, chunk), lambda c: (0, c))
    block_spec = pl.BlockSpec(block.shape, lambda c: (0, 0, 0))
    return pl.pallas_call(
        functools.partial(fourier_kernel, adjoint, levels, fields),
        grid=(longitudes // chunk,),
        in_specs=[
            block_spec,
            pl.BlockSpec(scale.shape, lambda c: (0, 0)),
            pl.BlockSpec(weight.shape, lambda c: (0, 0)),
            table_spec,
            table_spec,
            coef_spec,
            coef_spec,
        ],
        out_specs=block_spec,
        out_shape=jax.ShapeDtypeStruct(block.shape, f32),
        scratch_shapes=[
            pltpu.VMEM((before, slots2), f32),
            pltpu.VMEM((before, chunk), f32),
            pltpu.VMEM((after, chunk), f32),
            pltpu.VMEM((after, slots2), f32),
        ],
        compiler_params=pltpu.CompilerParams(vmem_limit_bytes=40 * 1024 * 1024),
        name="adjoint" if adjoint else "forward",
    )(block, scale, weight, high, low, value, zonal)


def body(
    right_vector, left_prev, beta_prev, kept_vectors, kept_count, wave_table, legendre,
    quad_weights, coef_value, coef_zonal,
):
    levels, fields, waves_dev, _, degrees = right_vector.shape
    lat_dev, longitudes = coef_value.shape[2:]
    groups = lax.axis_size("wave")
    keep_count = kept_vectors.shape[0]
    entries = float(right_vector.size * groups * lax.axis_size("field"))
    device = lax.axis_index("wave")
    own_waves = lax.dynamic_slice_in_dim(wave_table, device * waves_dev, waves_dev)
    own_weights = lax.dynamic_slice_in_dim(quad_weights, device * lat_dev, lat_dev)
    weight = (own_weights * (degrees * longitudes) ** -0.5)[:, None]
    scale = (wave_table.astype(f32) / degrees)[None, :]
    table = fourier_table(wave_table, longitudes)
    degree_ids = jnp.arange(degrees, dtype=jnp.int32)
    live_mask = (degree_ids[None, :] >= own_waves[:, None]).astype(f32)[None, None, :, None, :]
    right_live = right_vector * live_mask

    def exchange(x):
        return lax.all_to_all(
            x.reshape(groups, lat_dev, -1), "wave", split_axis=0, concat_axis=0, tiled=True
        )

    def grid_pass(adjoint, latitude_part):
        block = exchange(latitude_part)
        block = fourier_call(
            adjoint, levels, fields, block, scale, weight, table, coef_value, coef_zonal
        )
        return exchange(block).reshape(groups * lat_dev, -1)

    (part,) = legendre_call("synthesis", own_waves, beta_prev, legendre, right_vector)
    image = grid_pass(False, part)
    residual_left, part = legendre_call(
        "both", own_waves, beta_prev, legendre, right_vector, left_prev, image
    )
    image = grid_pass(True, part)
    (adjoint_raw,) = legendre_call(
        "analysis", own_waves, beta_prev, legendre, residual_left, None, image
    )

    def project(vector):
        return jnp.sum(kept_vectors.astype(f32) * vector[None], axis=(1, 2, 3, 4, 5))

    sums = jnp.concatenate(
        [
            jnp.sum(residual_left * residual_left)[None],
            project(adjoint_raw),
            project(right_live),
        ]
    )
    sums = lax.psum(sums, ("wave", "field")) / entries
    alpha = jnp.sqrt(sums[0] + epsilon)
    live_flags = (jnp.arange(keep_count, dtype=jnp.int32) < kept_count[0]).astype(f32)
    correlations = (
        sums[1 : 1 + keep_count] / alpha - alpha * sums[1 + keep_count :]
    ) * live_flags
    correction = jnp.sum(
        kept_vectors.astype(f32) * correlations[:, None, None, None, None, None], axis=0
    )
    orthogonal = adjoint_raw / alpha - alpha * right_live - live_mask * correction
    square = lax.psum(jnp.sum(orthogonal * orthogonal), ("wave", "field")) / entries
    beta = jnp.sqrt(square + epsilon)
    return (residual_left / alpha, orthogonal / beta, correlations, jnp.stack([alpha, beta]))


def solution(mesh):
    spectral = P("field", None, "wave", None, None)
    grid = P(None, None, "wave", None)
    return jax.shard_map(
        body,
        mesh=mesh,
        in_specs=(
            spectral,
            spectral,
            P(),
            P(None, "field", None, "wave", None, None),
            P(),
            P(),
            P("wave", None, None),
            P(),
            grid,
            grid,
        ),
        out_specs=(spectral, spectral, P(), P()),
        check_vma=False,
    )
```

```python
import functools
import math

import jax
import jax.numpy as jnp
from jax import lax
from jax.experimental import pallas as pl
from jax.experimental.pallas import tpu as pltpu
from jax.sharding import PartitionSpec as P

time_step = 0.5
epsilon = 1e-06
f32 = jnp.float32
bf16 = jnp.bfloat16


def split(x):
    high = x.astype(bf16)
    return high, (x - high.astype(f32)).astype(bf16)


def dot(a, b, contract):
    return lax.dot_general(a, b, (((1,), (contract,)), ((), ())), preferred_element_type=f32)


def split_dot(rows, b_high, b_low, contract):
    count = rows.shape[0]
    high = rows.astype(bf16).astype(f32)
    both = jnp.concatenate([high, rows - high], axis=0).astype(bf16)
    upper = dot(both, b_high, contract)
    lower = dot(both[:count], b_low, contract)
    return upper[:count] + (upper[count:] + lower)


def table_kernel(longitudes, waves_ref, high_ref, low_ref):
    _, rows, width = high_ref.shape
    column = lax.broadcasted_iota(jnp.int32, (rows, width), 1)
    phase = waves_ref[...] * column
    if longitudes & (longitudes - 1):
        phase = lax.rem(phase, longitudes)
    turn = phase.astype(f32) * (4.0 / longitudes)
    quadrant = jnp.floor(turn + 0.5)
    angle = (turn - quadrant) * (0.5 * math.pi)
    quadrant = quadrant.astype(jnp.int32) & 3
    square = angle * angle
    sine = angle * (
        1.0 + square * (-1 / 6 + square * (1 / 120 + square * (-1 / 5040 + square / 362880)))
    )
    cosine = 1.0 + square * (
        -0.5 + square * (1 / 24 + square * (-1 / 720 + square * (1 / 40320 - square / 3628800)))
    )
    odd = (quadrant & 1) == 1
    turned = jnp.where(odd, sine, cosine)
    turned = jnp.where((quadrant == 1) | (quadrant == 2), -turned, turned)
    minus_sine = jnp.where(odd, cosine, sine)
    minus_sine = jnp.where(quadrant < 2, -minus_sine, minus_sine)
    for r, value in enumerate((turned, minus_sine)):
        high, low = split(value)
        high_ref[r] = high
        low_ref[r] = low


def fourier_table(wave_table, longitudes):
    slots = wave_table.shape[0]
    block = slots // 4
    out = jax.ShapeDtypeStruct((2, slots, longitudes), bf16)
    parts = pl.pallas_call(
        functools.partial(table_kernel, longitudes),
        grid=(4,),
        in_specs=[pl.BlockSpec((block, 1), lambda i: (i, 0))],
        out_specs=[pl.BlockSpec((2, block, longitudes), lambda i: (0, i, 0))] * 2,
        out_shape=[out, out],
        name="table",
    )(wave_table[:, None])
    return [part.reshape(2 * slots, longitudes) for part in parts]


def loop(count, visit):
    def at(index, carry):
        visit(index)
        return carry

    lax.fori_loop(1, count, at, 0)


def exchange_kernel(blocks, sums, *refs):
    refs = list(refs)
    block_ref = refs.pop(0) if blocks else None
    row_ref = refs.pop(0) if sums else None
    out_ref = refs.pop(0) if blocks else None
    total_ref = refs.pop(0) if sums else None
    wave, field = lax.axis_index("wave"), lax.axis_index("field")
    groups, cores = lax.axis_size("wave"), lax.axis_size("field")
    count = groups * cores
    me = wave * cores + field

    def device(index):
        return {"wave": lax.div(index, cores), "field": lax.rem(index, cores)}

    barrier = pltpu.get_barrier_semaphore()
    if sums:
        loop(count, lambda d: pl.semaphore_signal(
            barrier, inc=1, device_id=device(lax.rem(me + d, count)),
            device_id_type=pl.DeviceIdType.MESH))
        pl.semaphore_wait(barrier, count - 1)
    else:
        loop(groups, lambda d: pl.semaphore_signal(
            barrier, inc=1, device_id={"wave": lax.rem(wave + d, groups)},
            device_id_type=pl.DeviceIdType.MESH))
        pl.semaphore_wait(barrier, groups - 1)
    if sums:
        slots, row_send, row_recv = refs[-3:]

        def row_copy(peer, slot):
            return pltpu.make_async_remote_copy(
                src_ref=row_ref, dst_ref=slots.at[slot], send_sem=row_send.at[peer],
                recv_sem=row_recv.at[slot], device_id=device(peer),
                device_id_type=pl.DeviceIdType.MESH)

        loop(count, lambda d: row_copy(lax.rem(me + d, count), me).start())
    if blocks:
        local, send, recv = refs[:3]

        def block_copy(peer, slot):
            return pltpu.make_async_remote_copy(
                src_ref=block_ref.at[peer], dst_ref=out_ref.at[slot], send_sem=send.at[peer],
                recv_sem=recv.at[slot], device_id={"wave": peer},
                device_id_type=pl.DeviceIdType.MESH)

        loop(groups, lambda d: block_copy(lax.rem(wave + d, groups), wave).start())
        own = pltpu.make_async_copy(block_ref.at[wave], out_ref.at[wave], local)
        own.start()
    if sums:
        slots[me] = row_ref[...]

        def row_wait(d):
            peer = lax.rem(me + d, count)
            row_copy(peer, peer).wait_recv()
            row_copy(peer, peer).wait_send()

        loop(count, row_wait)
        total_ref[...] = jnp.sum(slots[...], axis=0)
    if blocks:

        def block_wait(d):
            peer = lax.rem(wave + d, groups)
            block_copy(peer, peer).wait_recv()
            block_copy(peer, peer).wait_send()

        loop(groups, block_wait)
        own.wait()


def exchange_call(identity, block=None, sums=None):
    groups, cores = lax.axis_size("wave"), lax.axis_size("field")
    operands, in_specs, out_specs, out_shape, scratch = [], [], [], [], []
    if block is not None:
        operands.append(block)
        in_specs.append(pl.BlockSpec(memory_space=pl.ANY))
        out_specs.append(pl.BlockSpec(memory_space=pl.ANY))
        out_shape.append(jax.ShapeDtypeStruct(block.shape, f32))
        scratch += [
            pltpu.SemaphoreType.DMA,
            pltpu.SemaphoreType.DMA((groups,)),
            pltpu.SemaphoreType.DMA((groups,)),
        ]
    if sums is not None:
        row = jnp.pad(sums, (0, 128 - sums.shape[0]))[None]
        operands.append(row)
        in_specs.append(pl.BlockSpec(memory_space=pltpu.VMEM))
        out_specs.append(pl.BlockSpec(memory_space=pltpu.VMEM))
        out_shape.append(jax.ShapeDtypeStruct(row.shape, f32))
        scratch += [
            pltpu.VMEM((groups * cores,) + row.shape, f32),
            pltpu.SemaphoreType.DMA((groups * cores,)),
            pltpu.SemaphoreType.DMA((groups * cores,)),
        ]
    return pl.pallas_call(
        functools.partial(exchange_kernel, block is not None, sums is not None),
        in_specs=in_specs,
        out_specs=out_specs,
        out_shape=out_shape,
        scratch_shapes=scratch,
        compiler_params=pltpu.CompilerParams(collective_id=identity, has_side_effects=True),
        name=f"exchange_{identity}",
    )(*operands)


def legendre_kernel(mode, block, waves_ref, beta_ref, *refs):
    refs = list(refs)
    basis_ref = refs.pop(0)
    spectral_ref = refs.pop(0)
    prev_ref = refs.pop(0) if mode != "synthesis" else None
    image_ref = refs.pop(0) if mode != "synthesis" else None
    new_ref = refs.pop(0) if mode != "synthesis" else None
    out_ref = refs.pop(0) if mode != "analysis" else None
    rows_ref = refs.pop(0)
    gather_ref = refs.pop(0) if mode != "synthesis" else None
    acc_ref = refs.pop(0) if mode != "analysis" else None
    levels, fields = spectral_ref.shape[:2]
    parts = spectral_ref.shape[3]
    degrees = basis_ref.shape[1]
    used = levels * fields * parts
    step = pl.program_id(0)
    waves_dev = pl.num_programs(0) * block

    @pl.when(step == 0)
    def _():
        rows_ref[...] = jnp.zeros_like(rows_ref)
        if gather_ref is not None:
            gather_ref[...] = image_ref[...].T

    for j in range(block):
        slot = step * block + j
        degree = lax.broadcasted_iota(jnp.int32, (rows_ref.shape[1], degrees), 1)
        mask = (degree >= waves_ref[slot]).astype(f32)

        def pack(which, ref):
            for l in range(levels):
                for f in range(fields):
                    at = (l * fields + f) * parts
                    rows_ref[which, pl.ds(at, parts), :] = ref[l, f, j]

        pack(0, spectral_ref)
        current = rows_ref[0] * mask
        high, low = split(basis_ref[j])
        if mode != "synthesis":
            for i in range(used):
                rows_ref[1, pl.ds(i, 1), :] = gather_ref[pl.ds(i * waves_dev + slot, 1), :]
            image = split_dot(rows_ref[1], high, low, 1) * mask
            current = current + time_step * image
            pack(2, prev_ref)
            if mode == "both":
                current = current - beta_ref[0] * (rows_ref[2] * mask)
            else:
                current = current / beta_ref[0] - beta_ref[0] * (rows_ref[2] * mask)
            for l in range(levels):
                for f in range(fields):
                    at = (l * fields + f) * parts
                    new_ref[l, f, j] = current[at : at + parts]
        if mode != "analysis":
            result = split_dot(current, high, low, 0)
            for i in range(used):
                acc_ref[pl.ds(i * waves_dev + slot, 1), :] = result[i : i + 1]

    if mode != "analysis":

        @pl.when(step == pl.num_programs(0) - 1)
        def _():
            out_ref[...] = acc_ref[...].T


def legendre_call(mode, waves, beta, basis, spectral, prev=None, image=None):
    levels, fields, waves_dev, parts, degrees = spectral.shape
    latitudes = basis.shape[2]
    used = levels * fields * parts
    padded = -(-used // 16) * 16
    block = 2 if waves_dev % 2 == 0 else 1
    spec = pl.BlockSpec((levels, fields, block, parts, degrees), lambda s, *_: (0, 0, s, 0, 0))
    whole = pl.BlockSpec((latitudes, used * waves_dev), lambda s, *_: (0, 0))
    operands = [basis, spectral]
    in_specs = [pl.BlockSpec((block, degrees, latitudes), lambda s, *_: (s, 0, 0)), spec]
    out_specs, out_shape = [], []
    scratch = [pltpu.VMEM((3, padded, degrees), f32)]
    lanes = pltpu.VMEM((used * waves_dev, latitudes), f32)
    if mode != "synthesis":
        operands.append(prev)
        in_specs.append(spec)
    if mode != "synthesis":
        operands.append(image)
        in_specs.append(whole)
        out_specs.append(spec)
        out_shape.append(jax.ShapeDtypeStruct(spectral.shape, f32))
        scratch.append(lanes)
    if mode != "analysis":
        out_specs.append(whole)
        out_shape.append(jax.ShapeDtypeStruct((latitudes, used * waves_dev), f32))
        scratch.append(lanes)
    return pl.pallas_call(
        functools.partial(legendre_kernel, mode, block),
        grid_spec=pltpu.PrefetchScalarGridSpec(
            num_scalar_prefetch=2,
            grid=(waves_dev // block,),
            in_specs=in_specs,
            out_specs=out_specs,
            scratch_shapes=scratch,
        ),
        out_shape=out_shape,
        compiler_params=pltpu.CompilerParams(vmem_limit_bytes=40 * 1024 * 1024),
        name=mode,
    )(waves, beta, *operands)


def fourier_kernel(
    adjoint, levels, fields, block_ref, scale_ref, weight_ref, high_ref, low_ref, value_ref,
    zonal_ref, out_ref, coef_ref, left_ref, right_ref, acc_ref,
):
    groups, lat_dev, columns = block_ref.shape
    items = levels * fields
    waves_dev = columns // (2 * items)
    slots = groups * waves_dev
    rows = items * lat_dev
    step = pl.program_id(0)

    @pl.when(step == 0)
    def _():
        for w in range(groups):
            for i in range(items):
                for r in range(2):
                    coef_ref[
                        pl.ds(i * lat_dev, lat_dev), pl.ds(r * slots + w * waves_dev, waves_dev)
                    ] = block_ref[w, :, pl.ds((2 * i + r) * waves_dev, waves_dev)]
        if not adjoint:
            scale = scale_ref[...]
            coef_ref[pl.ds(rows, rows), pl.ds(0, slots)] = (
                -scale * coef_ref[pl.ds(0, rows), pl.ds(slots, slots)]
            )
            coef_ref[pl.ds(rows, rows), pl.ds(slots, slots)] = (
                scale * coef_ref[pl.ds(0, rows), pl.ds(0, slots)]
            )
        acc_ref[...] = jnp.zeros_like(acc_ref)

    high, low = high_ref[...], low_ref[...]
    left_ref[...] = split_dot(coef_ref[...], high, low, 0)
    weight = weight_ref[...]
    for l in range(levels):
        base = l * fields
        if adjoint:
            grid = [left_ref[pl.ds((base + f) * lat_dev, lat_dev), :] * weight for f in range(fields)]
            for g in range(fields):
                for k, ref in enumerate((value_ref, zonal_ref)):
                    total = sum(ref[f, g].astype(f32) * grid[f] for f in range(fields))
                    right_ref[pl.ds(k * rows + (base + g) * lat_dev, lat_dev), :] = total
        else:
            value = [left_ref[pl.ds((base + g) * lat_dev, lat_dev), :] for g in range(fields)]
            slope = [left_ref[pl.ds(rows + (base + g) * lat_dev, lat_dev), :] for g in range(fields)]
            for f in range(fields):
                total = sum(
                    value_ref[f, g].astype(f32) * value[g] + zonal_ref[f, g].astype(f32) * slope[g]
                    for g in range(fields)
                )
                right_ref[pl.ds((base + f) * lat_dev, lat_dev), :] = total * weight
    acc_ref[...] += split_dot(right_ref[...], high, low, 1)

    @pl.when(step == pl.num_programs(0) - 1)
    def _():
        if adjoint:
            scale = scale_ref[...]
            first = pl.ds(0, rows)
            second = pl.ds(rows, rows)
            acc_ref[first, pl.ds(0, slots)] += scale * acc_ref[second, pl.ds(slots, slots)]
            acc_ref[first, pl.ds(slots, slots)] -= scale * acc_ref[second, pl.ds(0, slots)]
        for w in range(groups):
            for i in range(items):
                for r in range(2):
                    out_ref[w, :, pl.ds((2 * i + r) * waves_dev, waves_dev)] = acc_ref[
                        pl.ds(i * lat_dev, lat_dev), pl.ds(r * slots + w * waves_dev, waves_dev)
                    ]


def fourier_call(adjoint, levels, fields, block, scale, weight, table, value, zonal):
    groups, lat_dev, columns = block.shape
    high, low = table
    slots2, longitudes = high.shape
    chunk = 256
    rows = levels * fields * lat_dev
    before, after = (rows, 2 * rows) if adjoint else (2 * rows, rows)
    coef_spec = pl.BlockSpec((fields, fields, lat_dev, chunk), lambda c: (0, 0, 0, c))
    table_spec = pl.BlockSpec((slots2, chunk), lambda c: (0, c))
    block_spec = pl.BlockSpec(block.shape, lambda c: (0, 0, 0))
    return pl.pallas_call(
        functools.partial(fourier_kernel, adjoint, levels, fields),
        grid=(longitudes // chunk,),
        in_specs=[
            block_spec,
            pl.BlockSpec(scale.shape, lambda c: (0, 0)),
            pl.BlockSpec(weight.shape, lambda c: (0, 0)),
            table_spec,
            table_spec,
            coef_spec,
            coef_spec,
        ],
        out_specs=block_spec,
        out_shape=jax.ShapeDtypeStruct(block.shape, f32),
        scratch_shapes=[
            pltpu.VMEM((before, slots2), f32),
            pltpu.VMEM((before, chunk), f32),
            pltpu.VMEM((after, chunk), f32),
            pltpu.VMEM((after, slots2), f32),
        ],
        compiler_params=pltpu.CompilerParams(vmem_limit_bytes=40 * 1024 * 1024),
        name="adjoint" if adjoint else "forward",
    )(block, scale, weight, high, low, value, zonal)


def body(
    right_vector, left_prev, beta_prev, kept_vectors, kept_count, wave_table, legendre,
    quad_weights, coef_value, coef_zonal,
):
    levels, fields, waves_dev, _, degrees = right_vector.shape
    lat_dev, longitudes = coef_value.shape[2:]
    groups = lax.axis_size("wave")
    keep_count = kept_vectors.shape[0]
    entries = float(right_vector.size * groups * lax.axis_size("field"))
    device = lax.axis_index("wave")
    own_waves = lax.dynamic_slice_in_dim(wave_table, device * waves_dev, waves_dev)
    own_weights = lax.dynamic_slice_in_dim(quad_weights, device * lat_dev, lat_dev)
    weight = (own_weights * (degrees * longitudes) ** -0.5)[:, None]
    scale = (wave_table.astype(f32) / degrees)[None, :]
    table = fourier_table(wave_table, longitudes)
    degree_ids = jnp.arange(degrees, dtype=jnp.int32)
    live_mask = (degree_ids[None, :] >= own_waves[:, None]).astype(f32)[None, None, :, None, :]

    def grid_blocks(part):
        return part.reshape(groups, lat_dev, -1)

    def grid_pass(adjoint, block):
        return fourier_call(
            adjoint, levels, fields, block, scale, weight, table, coef_value, coef_zonal
        )

    (part,) = legendre_call("synthesis", own_waves, beta_prev, legendre, right_vector)
    (block,) = exchange_call(0, grid_blocks(part))
    (block,) = exchange_call(1, grid_pass(False, block))
    residual_left, part = legendre_call(
        "both", own_waves, beta_prev, legendre, right_vector, left_prev,
        block.reshape(groups * lat_dev, -1),
    )
    square = jnp.sum(residual_left * residual_left)[None]
    block, sums = exchange_call(2, grid_blocks(part), square)
    alpha = jnp.sqrt(sums[0, 0] / entries + epsilon)
    (block,) = exchange_call(3, grid_pass(True, block))
    (candidate,) = legendre_call(
        "analysis", own_waves, alpha[None], legendre, residual_left, right_vector,
        block.reshape(groups * lat_dev, -1),
    )
    raw = jnp.sum(kept_vectors.astype(f32) * candidate[None], axis=(1, 2, 3, 4, 5))
    (sums,) = exchange_call(4, sums=raw)
    live_flags = (jnp.arange(keep_count, dtype=jnp.int32) < kept_count[0]).astype(f32)
    correlations = sums[0, :keep_count] / entries * live_flags
    correction = jnp.sum(
        kept_vectors.astype(f32) * correlations[:, None, None, None, None, None], axis=0
    )
    orthogonal = candidate - live_mask * correction
    (sums,) = exchange_call(5, sums=jnp.sum(orthogonal * orthogonal)[None])
    beta = jnp.sqrt(sums[0, 0] / entries + epsilon)
    return (residual_left / alpha, orthogonal / beta, correlations, jnp.stack([alpha, beta]))


def solution(mesh):
    spectral = P("field", None, "wave", None, None)
    grid = P(None, None, "wave", None)
    return jax.shard_map(
        body,
        mesh=mesh,
        in_specs=(
            spectral,
            spectral,
            P(),
            P(None, "field", None, "wave", None, None),
            P(),
            P(),
            P("wave", None, None),
            P(),
            grid,
            grid,
        ),
        out_specs=(spectral, spectral, P(), P()),
        check_vma=False,
    )
```
